512 devices in a mesh: gr: 16 (over y, z_hi), gc: 32 (over z_lo, x, core).
Axes of the slice: x: 4, y: 4, z: 16 (z_hi: 4, z_lo: 4; z = z_hi * 4 + z_lo), core: 2. Of those that a mesh axis runs over, the one named last changes fastest.
Arguments:
- phase: bfloat16 [2, 12288, 2048], P(None, 'gr', 'gc'), may hold values from -0.59765625 to 0.59765625
- data: bfloat16 [2, 2048, 128], P(None, 'gc'), may hold values from -6 to 6
- column_ids: int32 [2048], replicated, may hold values from 0 to 8191
- noise_weight: float32 [8192], replicated, may hold values from 0.3 to 3
Outputs:
- fisher: float32 [12288, 12288], P('gr', 'gc')
- dirty_maps: float32 [12288, 128], P(('gr', 'gc'))
The draws below stay inside these ranges and needn't reach their ends.
All inputs are finite; a program needn't handle non-finite values.
Results may differ from the reference program's by a relative error of at most 0.0029.
Values may be sent and summed in bfloat16 or wider, within the bound.
No kernel may reach another device: no remote copies, remote signals or barrier semaphores. Data moves between devices by JAX's collectives and lax.ppermute only.
A program may use at most 64 MiB of HBM per device.

```python
import math
import jax
import jax.numpy as jnp
from jax import lax

P_SIZE = 12288
M = 128
SF = 8192
K = 2048


def plant(entries, key, low, high):
    extent = entries.shape
    spot = [jax.random.randint(jax.random.fold_in(key, axis), (), 0, extent[axis]) for axis in range(len(extent))]
    entries = entries.at[tuple(spot)].set(low)
    longest = extent.index(max(extent))
    spot[longest] = (spot[longest] + 1) % extent[longest]
    return entries.at[tuple(spot)].set(high)


def strengthened(values, key, source, target, blocks, factor):
    owner, partner = [(jnp.arange(values.shape[dim]) // (values.shape[dim] // blocks)).reshape([-1 if axis == dim else 1 for axis in range(values.ndim)]) for dim in (source, target)]
    chosen = jax.random.permutation(key, blocks)[partner]
    strong = (owner == chosen) | (owner == (partner + blocks // 2) % blocks)
    return jnp.where(strong, factor * values, values)


def level_of(key, dims, pieces, least, high):
    gain = 1.0
    for axis_at, shards_of in pieces:
        steps = jax.random.uniform(jax.random.fold_in(jax.random.fold_in(key, 6), axis_at), (shards_of,), jnp.float32, least / len(pieces), high / len(pieces))
        gain = gain * jnp.repeat(jnp.exp(steps), dims[axis_at] // shards_of).reshape((-1,) + (1,) * (len(dims) - 1 - axis_at))
    return gain


def normal_values(stream_key, extent, deviation, limit, shards=(), kind=jnp.bfloat16):
    entries = deviation * jax.random.normal(stream_key, extent, jnp.float32)
    if shards:
        entries = entries * level_of(stream_key, extent, shards, -0.22, 0.18)
    return jnp.clip(entries, -limit, limit).astype(kind)


def bell_draw_with(rng, extent, scale, most, cuts, heavy, kind=jnp.bfloat16):
    drawn = scale * jax.random.normal(rng, extent, jnp.float32)
    if cuts:
        drawn = drawn * level_of(rng, extent, cuts, -0.22, 0.18)
    return jnp.clip(strengthened(drawn, jax.random.fold_in(rng, 3), *heavy), -most, most).astype(kind)


def setup_inputs(seed: int = 0) -> dict:
    key_of = jax.random.split(jax.random.key(seed), 5)
    phase = bell_draw_with(key_of[0], (2, P_SIZE, K), 0.1, 0.59765625, ((1, 16), (2, 32)), (2, 1, 32, 2.75))
    data = normal_values(key_of[1], (2, K, M), 1.0, 6.0, ((1, 32),))
    column_ids = plant(jax.random.randint(key_of[2], (K,), 0, SF), jax.random.fold_in(key_of[2], 1), 0, SF - 1).astype(jnp.int32)
    noise_weight = jnp.clip(jnp.exp(jax.random.uniform(key_of[3], (SF,), jnp.float32, math.log(0.3), math.log(3.0))), 0.3, 3.0)
    return {"phase": phase, "data": data, "column_ids": column_ids, "noise_weight": noise_weight}


def reference(phase, data, column_ids, noise_weight):
    weight = jnp.take(noise_weight, column_ids.astype(jnp.int32))
    weighted = (phase.astype(jnp.float32) * weight).astype(jnp.bfloat16)
    left_flat = jnp.concatenate([phase[0], phase[1]], axis=1)
    right_flat = jnp.concatenate([weighted[0], weighted[1]], axis=1)
    fisher = lax.dot_general(left_flat, right_flat, (((1,), (1,)), ((), ())), preferred_element_type=jnp.float32)
    data_flat = jnp.concatenate([data[0], data[1]], axis=0)
    dirty_maps = jnp.dot(right_flat, data_flat, preferred_element_type=jnp.float32)
    return fisher, dirty_maps
```

```python
import itertools

import jax
import jax.numpy as jnp
from jax import lax
from jax.sharding import Mesh, PartitionSpec as P

AXES = ("y", "zh", "zl", "x", "c")


def turned(other_core):
    pairs = []
    for source, (y, zh, zl, x, c) in enumerate(itertools.product(range(4), range(4), range(4), range(4), range(2))):
        core = 1 - c if other_core else c
        pairs.append((source, (((zl * 4 + x) * 4 + y) * 4 + zh) * 2 + core))
    return pairs


def shards(phase, data, column_ids, noise_weight):
    core = lax.axis_index("c")
    group = (lax.axis_index("zl") * 4 + lax.axis_index("x")) * 2 + core
    rows, cols = phase.shape[1], phase.shape[2]
    half = rows // 2
    local = jnp.transpose(phase, (0, 2, 1))
    mine = lax.dynamic_slice_in_dim(local, core * half, half, 2)
    other = lax.dynamic_slice_in_dim(local, (1 - core) * half, half, 2)
    mine = lax.ppermute(mine, AXES, turned(False))
    other = lax.ppermute(other, AXES, turned(True))
    first = jnp.where(core == 0, mine, other)
    second = jnp.where(core == 0, other, mine)
    pair = jnp.stack([first, second])
    left = lax.all_gather(local, ("zl", "x", "c"), axis=0)
    across = lax.all_gather(pair, "zh", axis=0)
    pieces = [lax.all_gather(across[k], "y", axis=0) for k in range(4)]
    right = jnp.stack(pieces, axis=1)
    weight = jnp.take(noise_weight, column_ids, mode="clip").reshape(4, 4, 2, 1, cols, 1)
    right = (right.astype(jnp.float32) * weight).astype(jnp.bfloat16)
    fisher = lax.dot_general(
        left.reshape(-1, rows), right.reshape(-1, half), (((0,), (0,)), ((), ())), preferred_element_type=jnp.float32
    )
    local_weight = lax.dynamic_slice_in_dim(weight.reshape(-1), group * cols, cols, 0)
    weighted = (local.astype(jnp.float32) * local_weight[:, None]).astype(jnp.bfloat16)
    partial = lax.dot_general(
        weighted, data, (((0, 1), (0, 1)), ((), ())), preferred_element_type=jnp.float32
    )
    partial = partial.reshape(32, rows // 32, -1)
    parts = lax.all_to_all(partial, ("zl", "x", "c"), 0, 0)
    dirty_maps = jnp.sum(parts, axis=0)
    return fisher, dirty_maps


def solution(mesh):
    fine = Mesh(mesh.devices.reshape(4, 4, 4, 4, 2), AXES)
    return jax.shard_map(
        shards,
        mesh=fine,
        in_specs=(P(None, ("y", "zh"), ("zl", "x", "c")), P(None, ("zl", "x", "c"), None), P(), P()),
        out_specs=(P(("y", "zh"), ("zl", "x", "c")), P(AXES, None)),
        check_vma=False,
    )
```

```python
import jax
import jax.numpy as jnp
from jax import lax
from jax.sharding import Mesh, PartitionSpec as P

AXES = ("y", "zh", "zl", "x", "c")


def send(block, axis, step):
    return lax.ppermute(block, axis, [(i, (i + step) % 4) for i in range(4)])


def gather(block, axis):
    return lax.all_gather(block, axis, axis=0)


def table_rows(noise_weight, column_ids):
    table = noise_weight.reshape(-1, 128)
    high, low = column_ids >> 7, column_ids & 127
    pick = (lax.broadcasted_iota(jnp.int32, (table.shape[0], high.shape[0]), 0) == high[None]).astype(jnp.float32)
    lanes = lax.dot_general(
        table, pick, (((0,), (0,)), ((), ())), precision=lax.Precision.HIGHEST, preferred_element_type=jnp.float32
    )
    keep = lax.broadcasted_iota(jnp.int32, lanes.shape, 0) == low[None]
    return jnp.sum(jnp.where(keep, lanes, 0.0), axis=0)


def step(phase, data, column_ids, noise_weight):
    core = lax.axis_index("c")
    zl, x = lax.axis_index("zl"), lax.axis_index("x")
    rows, cols = phase.shape[1], phase.shape[2]
    half = rows // 2
    local = jnp.transpose(phase, (0, 2, 1))
    own = lax.ppermute(local, ("y", "zl"), [(4 * i + j, 4 * j + i) for i in range(4) for j in range(4)])
    line = gather(jnp.concatenate([local, data], axis=2), "zl")
    xprev = send(line, "x", 1)
    xsucc = send(line, "x", -1)
    xfar = send(line, "x", 2)
    across = gather(own, "zh")
    line, across = lax.optimization_barrier((line, across))
    spread = jnp.stack([across[..., :half], across[..., half:]], axis=1)
    spread = jnp.broadcast_to(spread, (4,) + spread.shape).reshape((32,) + spread.shape[2:])
    right = lax.all_to_all(spread, ("y", "x", "c"), 0, 0)
    weight = table_rows(noise_weight, column_ids).reshape(4, 4, 2, cols)
    left = jnp.zeros((4, 4, 2) + local.shape, jnp.bfloat16)
    seen = jnp.zeros((4, 4, 2) + data.shape, jnp.bfloat16)
    for offset, piece in ((0, line), (-1, xprev), (1, xsucc), (2, xfar)):
        place = (x + offset) % 4
        twin = lax.ppermute(piece, "c", [(0, 1), (1, 0)])
        for which, block in ((core, piece), (1 - core, twin)):
            block = block[:, None, None]
            left = lax.dynamic_update_slice(left, block[..., :rows], (0, place, which, 0, 0, 0))
            seen = lax.dynamic_update_slice(seen, block[..., rows:], (0, place, which, 0, 0, 0))
    over = (((0,), (0,)), ((), ()))
    share = rows // 32
    scale = weight.reshape(32, 1, cols, 1)
    first = ((zl * 4 + x) * 2 + core) * share
    mine = lax.dynamic_slice_in_dim(left.reshape(32, 2, cols, rows), first, share, 3)
    mine = (mine.astype(jnp.float32) * scale).astype(jnp.bfloat16).reshape(-1, share)
    dirty_maps = lax.dot_general(mine, seen.reshape(-1, data.shape[2]), over, preferred_element_type=jnp.float32)
    right = (right.astype(jnp.float32) * scale).astype(jnp.bfloat16).reshape(-1, half)
    fisher = lax.dot_general(left.reshape(-1, rows), right, over, preferred_element_type=jnp.float32)
    return fisher, dirty_maps


def solution(mesh):
    fine = Mesh(mesh.devices.reshape(4, 4, 4, 4, 2), AXES)
    return jax.shard_map(
        step,
        mesh=fine,
        in_specs=(P(None, ("y", "zh"), ("zl", "x", "c")), P(None, ("zl", "x", "c"), None), P(), P()),
        out_specs=(P(("y", "zh"), ("zl", "x", "c")), P(AXES, None)),
        check_vma=False,
    )
```

```python
import jax
import jax.numpy as jnp
from jax import lax
from jax.sharding import Mesh, PartitionSpec as P

AXES = ("y", "zh", "zl", "x", "c")


def send(block, axis, step):
    return lax.ppermute(block, axis, [(i, (i + step) % 4) for i in range(4)])


def gather(block, axis):
    return lax.all_gather(block, axis, axis=0)


def table_rows(noise_weight, column_ids):
    table = noise_weight.reshape(-1, 128)
    high, low = column_ids >> 7, column_ids & 127
    pick = (lax.broadcasted_iota(jnp.int32, (table.shape[0], high.shape[0]), 0) == high[None]).astype(jnp.float32)
    lanes = lax.dot_general(
        table, pick, (((0,), (0,)), ((), ())), precision=lax.Precision.HIGHEST, preferred_element_type=jnp.float32
    )
    keep = lax.broadcasted_iota(jnp.int32, lanes.shape, 0) == low[None]
    return jnp.sum(jnp.where(keep, lanes, 0.0), axis=0)


def step(phase, data, column_ids, noise_weight):
    core = lax.axis_index("c")
    zl, x = lax.axis_index("zl"), lax.axis_index("x")
    rows, cols = phase.shape[1], phase.shape[2]
    half = rows // 2
    local = jnp.transpose(phase, (0, 2, 1))
    line = gather(jnp.concatenate([local, data], axis=2), "zl")
    own = lax.all_to_all(line, "y", 0, 0)
    own = lax.dynamic_index_in_dim(own, zl, 0, keepdims=False)[..., :rows]
    own = jnp.transpose(own.reshape(2, cols, 2, half), (2, 0, 1, 3))
    xprev = send(line, "x", 1)
    xsucc = send(line, "x", -1)
    xfar = send(line, "x", 2)
    across = gather(own, "zh")
    line, across = lax.optimization_barrier((line, across))
    spread = jnp.broadcast_to(across, (4,) + across.shape).reshape((32,) + across.shape[2:])
    right = lax.all_to_all(spread, ("y", "x", "c"), 0, 0)
    weight = table_rows(noise_weight, column_ids).reshape(4, 4, 2, cols)
    left = jnp.zeros((4, 4, 2) + local.shape, jnp.bfloat16)
    seen = jnp.zeros((4, 4, 2) + data.shape, jnp.bfloat16)
    for offset, piece in ((0, line), (-1, xprev), (1, xsucc), (2, xfar)):
        place = (x + offset) % 4
        twin = lax.ppermute(piece, "c", [(0, 1), (1, 0)])
        for which, block in ((core, piece), (1 - core, twin)):
            block = block[:, None, None]
            left = lax.dynamic_update_slice(left, block[..., :rows], (0, place, which, 0, 0, 0))
            seen = lax.dynamic_update_slice(seen, block[..., rows:], (0, place, which, 0, 0, 0))
    over = (((0,), (0,)), ((), ()))
    share = rows // 32
    scale = weight.reshape(32, 1, cols, 1)
    first = ((zl * 4 + x) * 2 + core) * share
    mine = lax.dynamic_slice_in_dim(left.reshape(32, 2, cols, rows), first, share, 3)
    mine = (mine.astype(jnp.float32) * scale).astype(jnp.bfloat16).reshape(-1, share)
    dirty_maps = lax.dot_general(mine, seen.reshape(-1, data.shape[2]), over, preferred_element_type=jnp.float32)
    right = (right.astype(jnp.float32) * scale).astype(jnp.bfloat16).reshape(-1, half)
    fisher = lax.dot_general(left.reshape(-1, rows), right, over, preferred_element_type=jnp.float32)
    return fisher, dirty_maps


def solution(mesh):
    fine = Mesh(mesh.devices.reshape(4, 4, 4, 4, 2), AXES)
    return jax.shard_map(
        step,
        mesh=fine,
        in_specs=(P(None, ("y", "zh"), ("zl", "x", "c")), P(None, ("zl", "x", "c"), None), P(), P()),
        out_specs=(P(("y", "zh"), ("zl", "x", "c")), P(AXES, None)),
        check_vma=False,
    )
```

```python
import jax
import jax.numpy as jnp
from jax import lax
from jax.sharding import Mesh, PartitionSpec as P

AXES = ("y", "zh", "zl", "x", "c")


def send(block, axis, step):
    return lax.ppermute(block, axis, [(i, (i + step) % 4) for i in range(4)])


def gather(block, axis):
    return lax.all_gather(block, axis, axis=0)


def table_rows(noise_weight, column_ids):
    table = noise_weight.reshape(-1, 128)
    high, low = column_ids >> 7, column_ids & 127
    pick = (lax.broadcasted_iota(jnp.int32, (table.shape[0], high.shape[0]), 0) == high[None]).astype(jnp.float32)
    lanes = lax.dot_general(
        table, pick, (((0,), (0,)), ((), ())), precision=lax.Precision.HIGHEST, preferred_element_type=jnp.float32
    )
    keep = lax.broadcasted_iota(jnp.int32, lanes.shape, 0) == low[None]
    return jnp.sum(jnp.where(keep, lanes, 0.0), axis=0)


def step(phase, data, column_ids, noise_weight):
    core = lax.axis_index("c")
    zl, x = lax.axis_index("zl"), lax.axis_index("x")
    rows, cols = phase.shape[1], phase.shape[2]
    half = rows // 2
    local = jnp.transpose(phase, (0, 2, 1))
    line = gather(jnp.concatenate([local, data], axis=2), "zl")
    own = lax.all_to_all(line, "y", 0, 0)
    own = lax.dynamic_index_in_dim(own, zl, 0, keepdims=False)[..., :rows]
    own = jnp.transpose(own.reshape(2, cols, 2, half), (2, 0, 1, 3))
    xprev = send(line, "x", 1)
    xsucc = send(line, "x", -1)
    xfar = send(line, "x", 2)
    across = gather(own, "zh")
    line, across = lax.optimization_barrier((line, across))
    spread = jnp.broadcast_to(across[:, None], (4,) + across.shape).reshape((32,) + across.shape[2:])
    right = lax.all_to_all(spread, ("x", "y", "c"), 0, 0)
    weight = jnp.transpose(table_rows(noise_weight, column_ids).reshape(4, 4, 2, cols), (1, 0, 2, 3))
    left = jnp.zeros((4, 4, 2) + local.shape, jnp.bfloat16)
    seen = jnp.zeros((4, 4, 2) + data.shape, jnp.bfloat16)
    for offset, piece in ((0, line), (-1, xprev), (1, xsucc), (2, xfar)):
        place = (x + offset) % 4
        twin = lax.ppermute(piece, "c", [(0, 1), (1, 0)])
        for which, block in ((core, piece), (1 - core, twin)):
            block = block[None, :, None]
            left = lax.dynamic_update_slice(left, block[..., :rows], (place, 0, which, 0, 0, 0))
            seen = lax.dynamic_update_slice(seen, block[..., rows:], (place, 0, which, 0, 0, 0))
    over = (((0,), (0,)), ((), ()))
    share = rows // 32
    scale = weight.reshape(32, 1, cols, 1)
    first = ((zl * 4 + x) * 2 + core) * share
    mine = lax.dynamic_slice_in_dim(left.reshape(32, 2, cols, rows), first, share, 3)
    mine = (mine.astype(jnp.float32) * scale).astype(jnp.bfloat16).reshape(-1, share)
    dirty_maps = lax.dot_general(mine, seen.reshape(-1, data.shape[2]), over, preferred_element_type=jnp.float32)
    right = (right.astype(jnp.float32) * scale).astype(jnp.bfloat16).reshape(-1, half)
    fisher = lax.dot_general(left.reshape(-1, rows), right, over, preferred_element_type=jnp.float32)
    return fisher, dirty_maps


def solution(mesh):
    fine = Mesh(mesh.devices.reshape(4, 4, 4, 4, 2), AXES)
    return jax.shard_map(
        step,
        mesh=fine,
        in_specs=(P(None, ("y", "zh"), ("zl", "x", "c")), P(None, ("zl", "x", "c"), None), P(), P()),
        out_specs=(P(("y", "zh"), ("zl", "x", "c")), P(AXES, None)),
        check_vma=False,
    )
```
